32 devices in a mesh: row: 4 (over y, x), col: 8 (over z, core).
Axes of the slice: x: 2, y: 2, z: 4, core: 2. Of those that a mesh axis runs over, the one named last changes fastest.
Arguments:
- parent_entries: float32 [16384, 16384], P('row', 'col'), may hold values from -1.5 to 1.5
- children: float32 [6144, 12288], P('row', 'col'), may hold values from -1.5 to 1.5
- shift: float32 [16384], P('row'), may hold values from 24 to 48
- child_map: int32 [2, 96], replicated, may hold values from 0 to 255, as said below
Outputs:
- factored_front: float32 [16384, 16384], P('row', 'col')
The draws below stay inside these ranges and needn't reach their ends.
Inputs may be any that keep to these rules, and one draw needn't show every extreme that they name: `child_map`: row k sends child k's tiles to distinct parent tiles. For each child and each residue s modulo 4, the entries at positions congruent to s hold at most 8 values of any one residue modulo 4 and at most 8 of any one residue modulo 8, both bounds reached for every s; for each residue v modulo 4, exactly 24 entries of a row are congruent to v.
All inputs are finite; a program needn't handle non-finite values.
Results may differ from the reference program's by a relative error of at most 0.00005.
Values sent between devices are 32-bit elements; how exact they have to be, the bound alone decides.
A program may use at most 448 MiB of HBM per device.

```python
import math
import jax
import jax.numpy as jnp
from jax import lax

PARENT_ORDER = 16384
C = 6144
TILE = 64
ROWS_GRID = 4
COLS_GRID = 8
PBLOCKS = 256
CBLOCKS = 96
ELIMINATED_COLS = 512
GROUPS = 24
SLOTS = 8


def draw_child_map(key, part):
    rows_out = []
    ordinal = jnp.arange(CBLOCKS)
    group_of = ordinal // ROWS_GRID
    residue = ordinal % ROWS_GRID
    steps_idx = jnp.arange(GROUPS)
    spread = max(ROWS_GRID - 1, 1)
    for child in range(2):
        child_key = jax.random.fold_in(key, child + 11)
        key_lead, key_order, key_upper, key_slot = jax.random.split(child_key, 4)
        leading_row = jax.random.randint(key_lead, (), 0, ROWS_GRID)
        offsets = jnp.where(steps_idx < SLOTS, leading_row, (leading_row + 1 + (steps_idx - SLOTS) % spread) % ROWS_GRID)
        shuffle = jax.random.permutation(key_order, GROUPS)
        offset_of = offsets[shuffle]
        in_lead = shuffle < SLOTS
        dest_row = (residue + offset_of[group_of]) % ROWS_GRID
        upper_half = jax.random.randint(key_upper, (CBLOCKS,), 0, 2)
        upper_half = jnp.where(in_lead[group_of], 0, upper_half)
        dest_col = dest_row + ROWS_GRID * upper_half
        earlier = (dest_col[:, None] == dest_col[None, :]) & (ordinal[None, :] < ordinal[:, None])
        place_rank = jnp.sum(earlier.astype(jnp.int32), axis=1)
        levels = jax.random.permutation(key_slot, PBLOCKS // COLS_GRID)
        rows_out.append(levels[place_rank] * COLS_GRID + dest_col)
    return jnp.stack(rows_out).astype(jnp.int32)


def level_of(own_key, shape, cuts, smallest, high):
    def one(position, blocks):
        steps = jax.random.uniform(jax.random.fold_in(jax.random.fold_in(own_key, 6), position), (blocks,), jnp.float32, smallest / len(cuts), high / len(cuts))
        return jnp.repeat(jnp.exp(steps), shape[position] // blocks).reshape((-1,) + (1,) * (len(shape) - position - 1))

    factor_of = one(*cuts[0])
    for cut in cuts[1:]:
        factor_of = factor_of * one(*cut)
    return factor_of


def scatter_about(rng, extent, width, limit, cuts=(), kind=jnp.bfloat16):
    values = width * jax.random.normal(rng, extent, jnp.float32)
    if cuts:
        values = values * level_of(rng, extent, cuts, -0.22, 0.18)
    return jnp.clip(values, -limit, limit).astype(kind)


def setup_inputs(seed: int = 0) -> dict:
    streams_of = jax.random.split(jax.random.key(seed), 5)
    return {
        "parent_entries": scatter_about(streams_of[0], (PARENT_ORDER, PARENT_ORDER), 0.25, 1.5, ((0, 4), (1, 8)), jnp.float32),
        "children": scatter_about(streams_of[1], (C, 2 * C), 0.25, 1.5, ((0, 4), (1, 8)), jnp.float32),
        "shift": jnp.clip(jnp.exp(math.log(48.0) - 0.6931472 * jax.random.uniform(streams_of[2], (PARENT_ORDER,), jnp.float32) ** level_of(streams_of[2], (PARENT_ORDER,), ((0, 4),), -0.2, 0.2)), 24.0, 48.0),
        "child_map": draw_child_map(jax.random.fold_in(streams_of[4], 71), 0),
    }


def rows_natural(source, grid_size):
    count = source.shape[0]
    rest = source.shape[1:]
    shaped = source.reshape((grid_size, count // (grid_size * TILE), TILE) + rest)
    return jnp.swapaxes(shaped, 0, 1).reshape((count,) + rest)

def rows_storage(source, grid_size):
    count = source.shape[0]
    rest = source.shape[1:]
    shaped = source.reshape((count // (grid_size * TILE), grid_size, TILE) + rest)
    return jnp.swapaxes(shaped, 0, 1).reshape((count,) + rest)

def natural(source, row_grid, col_grid):
    return rows_natural(rows_natural(source, row_grid).T, col_grid).T

def storage(source, row_grid, col_grid):
    return rows_storage(rows_storage(source, row_grid).T, col_grid).T

def reference(parent_entries, children, shift, child_map):
    parent_front_matrix = natural(parent_entries, ROWS_GRID, COLS_GRID)
    diagonal = jnp.arange(PARENT_ORDER)
    parent_front_matrix = parent_front_matrix.at[diagonal, diagonal].add(rows_natural(shift, ROWS_GRID))
    front_tiles = parent_front_matrix.reshape(PBLOCKS, TILE, PBLOCKS, TILE)
    for child in range(2):
        block = natural(children[:, child * C:(child + 1) * C], ROWS_GRID, ROWS_GRID)
        child_tiles = block.reshape(CBLOCKS, TILE, CBLOCKS, TILE).transpose(0, 2, 1, 3)
        block_map = child_map[child]
        front_tiles = front_tiles.at[block_map[:, None], :, block_map[None, :], :].add(child_tiles)
    parent_front_matrix = front_tiles.reshape(PARENT_ORDER, PARENT_ORDER)
    leading_block = parent_front_matrix[:ELIMINATED_COLS, :ELIMINATED_COLS]
    pivot_block = jnp.linalg.cholesky((leading_block + leading_block.T) * 0.5)
    below_pivot_block = parent_front_matrix[ELIMINATED_COLS:, :ELIMINATED_COLS]
    lower_factor = jax.scipy.linalg.solve_triangular(pivot_block, below_pivot_block.T, lower=True).T
    schur_complement_block = parent_front_matrix[ELIMINATED_COLS:, ELIMINATED_COLS:] - jnp.dot(lower_factor, lower_factor.T, precision=lax.Precision.HIGHEST)
    upper_section = jnp.concatenate([pivot_block, jnp.zeros((ELIMINATED_COLS, PARENT_ORDER - ELIMINATED_COLS), jnp.float32)], axis=1)
    bottom_part = jnp.concatenate([lower_factor, schur_complement_block], axis=1)
    result = jnp.concatenate([upper_section, bottom_part], axis=0)
    return storage(result, ROWS_GRID, COLS_GRID)
```

```python
import jax
import jax.numpy as jnp
from jax import lax
from jax.experimental import pallas as pl
from jax.experimental.pallas import tpu as pltpu
from jax.sharding import PartitionSpec as P

TILE = 64
PAIR = 2 * TILE
LOOP_COLS = 2
LEADS = 2
LATE_CROSS = 16
BLOCK = 128
SMALL = pl.CostEstimate(flops=1, transcendentals=0, bytes_accessed=1024)


def params(mib):
    return pltpu.CompilerParams(vmem_limit_bytes=mib * 1024 * 1024)


def total(mask, value, axis):
    return jnp.sum(jnp.where(mask, value, 0), axis=axis)


def pick(value, index, axis=0):
    return lax.dynamic_index_in_dim(value, index, axis=axis, keepdims=False)


def flip(value, axis, distance):
    pairs = [(i, i ^ distance) for i in range(lax.axis_size(axis))]
    return lax.ppermute(value, axis, pairs)


def gather_flips(value, axis):
    size = lax.axis_size(axis)
    held = {0: value}
    distance = size // 2
    while distance > 1:
        for x in list(held):
            held[x ^ distance] = flip(held[x], axis, distance)
        distance //= 2
    even = jnp.stack([held[x] for x in range(0, size, 2)])
    return jnp.stack([even, flip(even, axis, 1)], axis=1).reshape((size,) + value.shape)


def unflip(value, index):
    size = value.shape[0]
    rest = value.shape[1:]
    for bit in range(size.bit_length() - 1):
        shaped = value.reshape((size >> (bit + 1), 2, 1 << bit) + rest)
        value = jnp.where((index >> bit) & 1 == 1, shaped[:, ::-1], shaped).reshape((size,) + rest)
    return value


def lane_half(value, column, half):
    return jnp.where(column % 2 == half, value, pltpu.roll(value, TILE, 1))


def lane_pair(column):
    return pl.ds(pl.multiple_of((column // 2) * PAIR, PAIR), PAIR)


def pack(sources, row_table, column_tables, rows):
    counts = [table.shape[0] for table in column_tables]
    widths = [source.shape[2] // TILE for source in sources]
    given = len(sources)

    def body(row_ref, column_ref, *refs):
        low = lax.broadcasted_iota(jnp.int32, (TILE, PAIR), 1) < TILE
        at = 0
        for out_ref, count in zip(refs[given:], counts):
            for first in range(0, count, 2):
                halves = []
                for half in range(2):
                    column = column_ref[at]
                    at += 1
                    value = refs[0][0, :, lane_pair(jnp.minimum(column, widths[0] - 1))]
                    start = widths[0]
                    for ref, width in zip(refs[1:given], widths[1:]):
                        place = jnp.clip(column - start, 0, width - 1)
                        value = jnp.where(column >= start, ref[0, :, lane_pair(place)], value)
                        start += width
                    halves.append(lane_half(value, column, half))
                out_ref[0, :, first * TILE : (first + 2) * TILE] = jnp.where(low, halves[0], halves[1])

    return pl.pallas_call(
        body,
        out_shape=[jax.ShapeDtypeStruct((rows, TILE, count * TILE), jnp.float32) for count in counts],
        grid_spec=pltpu.PrefetchScalarGridSpec(
            num_scalar_prefetch=2,
            grid=(rows,),
            in_specs=[
                pl.BlockSpec((1, TILE, source.shape[2]), lambda j, row, column: (row[j], 0, 0))
                for source in sources
            ],
            out_specs=[
                pl.BlockSpec((1, TILE, count * TILE), lambda j, row, column: (j, 0, 0)) for count in counts
            ],
        ),
        compiler_params=params(40),
        cost_estimate=SMALL,
    )(row_table, jnp.concatenate(column_tables), *sources)


def beside(arrived, row_table, got):
    rows, _, width = got.shape

    def body(row_ref, own_ref, got_ref, out_ref):
        out_ref[0, :, :width] = own_ref[0]
        out_ref[0, :, width:] = got_ref[0]

    return pl.pallas_call(
        body,
        out_shape=jax.ShapeDtypeStruct((rows, TILE, 2 * width), jnp.float32),
        grid_spec=pltpu.PrefetchScalarGridSpec(
            num_scalar_prefetch=1,
            grid=(rows,),
            in_specs=[
                pl.BlockSpec((1, TILE, width), lambda j, row: (row[j], 0, 0)),
                pl.BlockSpec((1, TILE, width), lambda j, row: (j, 0, 0)),
            ],
            out_specs=pl.BlockSpec((1, TILE, 2 * width), lambda j, row: (j, 0, 0)),
        ),
        compiler_params=params(32),
        cost_estimate=SMALL,
    )(row_table, arrived, got)


def chosen_rows(arrived, row_table):
    rows = row_table.shape[0]
    width = arrived.shape[2]

    def body(row_ref, in_ref, out_ref):
        out_ref[...] = in_ref[...]

    return pl.pallas_call(
        body,
        out_shape=jax.ShapeDtypeStruct((rows, TILE, width), jnp.float32),
        grid_spec=pltpu.PrefetchScalarGridSpec(
            num_scalar_prefetch=1,
            grid=(rows,),
            in_specs=[pl.BlockSpec((1, TILE, width), lambda j, row: (row[j], 0, 0))],
            out_specs=pl.BlockSpec((1, TILE, width), lambda j, row: (j, 0, 0)),
        ),
        compiler_params=params(32),
        cost_estimate=SMALL,
    )(row_table, arrived)


def extend_add(front, parts, row_table, column_tables, skip_rows, skip_cols):
    rows = row_table.shape[0]
    width = front.shape[1]
    columns = jnp.concatenate(column_tables)

    def body(row_ref, column_ref, front_ref, *refs):
        out_ref = refs[-1]
        out_ref[...] = front_ref[...]

        @pl.when(row_ref[pl.program_id(0)] >= skip_rows)
        def _():
            upper = lax.broadcasted_iota(jnp.int32, (TILE, PAIR), 1) // TILE
            at = 0
            for ref in refs[:-1]:
                for q in range(ref.shape[2] // TILE):
                    column = column_ref[at]
                    at += 1

                    @pl.when(column >= skip_cols)
                    def _():
                        first = (q // 2) * PAIR
                        value = lane_half(ref[0, :, first : first + PAIR], column, q % 2)
                        out_ref[:, lane_pair(column)] += jnp.where(upper == column % 2, value, 0.0)

    return pl.pallas_call(
        body,
        out_shape=jax.ShapeDtypeStruct(front.shape, jnp.float32),
        grid_spec=pltpu.PrefetchScalarGridSpec(
            num_scalar_prefetch=2,
            grid=(rows,),
            in_specs=[pl.BlockSpec((TILE, width), lambda j, row, column: (row[j], 0))]
            + [
                pl.BlockSpec((1, TILE, part.shape[2]), lambda j, row, column: (j, 0, 0))
                for part in parts
            ],
            out_specs=pl.BlockSpec((TILE, width), lambda j, row, column: (row[j], 0)),
        ),
        input_output_aliases={2: 0},
        compiler_params=params(32),
        cost_estimate=SMALL,
    )(row_table, columns, front, *parts)


def add_leads(panel, parts, row_tables, tables, kinds):
    rows = parts[0].shape[0]
    count = panel.shape[0] // TILE
    row_table = jnp.concatenate(row_tables)
    table = jnp.concatenate(tables)
    order = [t for kind in range(kinds) for t in range(kind, count, kinds)]

    def body(row_ref, table_ref, panel_ref, *refs):
        top_ref, turned_ref, work = refs[-3:]
        work[...] = panel_ref[...]
        low = lax.broadcasted_iota(jnp.int32, (TILE, PAIR), 1) < TILE
        for at, ref in enumerate(refs[:-3]):
            first = table_ref[2 * at] == 0
            second = table_ref[2 * at + 1] == 0

            @pl.when(first | second)
            def _():
                for j in range(rows):
                    place = pl.ds(pl.multiple_of(row_ref[at * rows + j] * TILE, TILE), TILE)
                    value = ref[j]
                    value = jnp.where(first, value, pltpu.roll(value, TILE, 1))
                    work[place, :] += jnp.where(low, value, 0.0)

        top_ref[...] = work[: kinds * TILE, :]
        for at in range(0, count, 2):
            pair = [work[t * TILE : (t + 1) * TILE, :] for t in order[at : at + 2]]
            turned_ref[:, at * TILE : (at + 2) * TILE] = jnp.concatenate(pair, axis=0).T[:TILE]

    smem = pl.BlockSpec(memory_space=pltpu.SMEM)
    vmem = pl.BlockSpec(memory_space=pltpu.VMEM)
    return pl.pallas_call(
        body,
        out_shape=(
            jax.ShapeDtypeStruct((kinds * TILE, PAIR), jnp.float32),
            jax.ShapeDtypeStruct((TILE, panel.shape[0]), jnp.float32),
        ),
        in_specs=[smem, smem, vmem] + [vmem] * len(parts),
        out_specs=(vmem, vmem),
        scratch_shapes=[pltpu.VMEM(panel.shape, jnp.float32)],
        compiler_params=params(40),
        cost_estimate=SMALL,
    )(row_table, table, panel, *parts)


def factor_and_inverse(matrix):
    size = matrix.shape[0]
    block = min(BLOCK, size)

    def dot(a, b, transposed=False):
        return lax.dot_general(
            a,
            b,
            (((1,), (1 if transposed else 0,)), ((), ())),
            precision=lax.Precision.HIGHEST,
            preferred_element_type=jnp.float32,
        )

    def body(matrix_ref, factor_ref, inverse_ref, work):
        lane = lax.broadcasted_iota(jnp.int32, (block, block), 1)
        deep = lax.broadcasted_iota(jnp.int32, (block, block), 0)
        wide_lane = lax.broadcasted_iota(jnp.int32, (1, 2 * block), 1)
        down = lax.broadcasted_iota(jnp.int32, (block, 1), 0)
        factor_ref[...] = jnp.zeros_like(factor_ref)
        inverse_ref[...] = jnp.zeros_like(inverse_ref)
        for start in range(0, size, block):
            end = start + block
            column = matrix_ref[start:, start:end]
            if start:
                column = column - dot(factor_ref[start:, :start], factor_ref[start:end, :start], True)
            work[:, :block] = column[:block]
            work[:, block:] = jnp.where(lane == deep, 1.0, 0.0)

            def step(j, carry):
                row = work[pl.ds(j, 1), :]
                held = work[...]
                scale = 1.0 / jnp.sqrt(jnp.sum(jnp.where(wide_lane == j, row, 0.0), axis=1, keepdims=True))
                row = row * scale
                below = jnp.sum(jnp.where(lane == j, held[:, :block], 0.0), axis=1, keepdims=True)
                below = jnp.where(down > j, below * scale, 0.0)
                work[...] = jnp.where(down == j, row, held - below * row)
                return carry

            lax.fori_loop(0, block, step, 0)
            diagonal_inverse = jnp.where(lane <= deep, work[:, block:], 0.0)
            factor_ref[start:end, start:end] = jnp.where(lane >= deep, work[:, :block], 0.0).T
            if end < size:
                factor_ref[end:, start:end] = dot(column[block:], diagonal_inverse, True)
            inverse_ref[start:end, start:end] = diagonal_inverse
            if start:
                row = dot(factor_ref[start:end, :start], inverse_ref[:start, :start])
                inverse_ref[start:end, :start] = -dot(diagonal_inverse, row)

    vmem = pl.BlockSpec(memory_space=pltpu.VMEM)
    shape = jax.ShapeDtypeStruct(matrix.shape, jnp.float32)
    return pl.pallas_call(
        body,
        out_shape=(shape, shape),
        in_specs=[vmem],
        out_specs=(vmem, vmem),
        scratch_shapes=[pltpu.VMEM((block, 2 * block), jnp.float32)],
        compiler_params=params(40),
        cost_estimate=SMALL,
    )(matrix)


def schur(parent, factor, factor_cols, panel_out, shift, place, grid_rows, grid_cols):
    rows_here, cols_here = parent.shape
    depth = factor.shape[1]
    step = min(4 * TILE, rows_here)
    lead = (grid_cols // grid_rows) * TILE

    def split(value):
        high = lax.reduce_precision(value, 8, 7)
        return high.astype(jnp.bfloat16), (value - high).astype(jnp.bfloat16)

    f_high, f_low = split(factor)
    c_high, c_low = split(factor_cols)

    def body(place_ref, parent_ref, fh_ref, fl_ref, ch_ref, cl_ref, panel_ref, shift_ref, out_ref):
        def dot(a, b):
            return jnp.dot(a[...], b[...], preferred_element_type=jnp.float32)

        update = dot(fh_ref, ch_ref) + dot(fl_ref, ch_ref) + dot(fh_ref, cl_ref)
        row = pl.program_id(0) * step + lax.broadcasted_iota(jnp.int32, (step, 1), 0)
        column = lax.broadcasted_iota(jnp.int32, (1, cols_here), 1)
        row_id = ((row // TILE) * grid_rows + place_ref[0]) * TILE + row % TILE
        column_id = ((column // TILE) * grid_cols + place_ref[1]) * TILE + column % TILE
        value = parent_ref[...] - update + jnp.where(row_id == column_id, shift_ref[...], 0.0)
        out_ref[...] = jnp.where(row < lead, 0.0, value)
        first = jnp.where(
            lax.broadcasted_iota(jnp.int32, (step, PAIR), 1) < TILE, panel_ref[...], out_ref[:, :PAIR]
        )
        out_ref[:, :PAIR] = first

    whole = lambda j, place: (0, 0)
    block = lambda j, place: (j, 0)
    return pl.pallas_call(
        body,
        out_shape=jax.ShapeDtypeStruct(parent.shape, jnp.float32),
        grid_spec=pltpu.PrefetchScalarGridSpec(
            num_scalar_prefetch=1,
            grid=(rows_here // step,),
            in_specs=[
                pl.BlockSpec((step, cols_here), block),
                pl.BlockSpec((step, depth), block),
                pl.BlockSpec((step, depth), block),
                pl.BlockSpec((depth, cols_here), whole),
                pl.BlockSpec((depth, cols_here), whole),
                pl.BlockSpec((step, PAIR), block),
                pl.BlockSpec((step, 1), block),
            ],
            out_specs=pl.BlockSpec((step, cols_here), block),
        ),
        compiler_params=params(50),
        cost_estimate=SMALL,
    )(place, parent, f_high, f_low, c_high, c_low, panel_out, shift[:, None])


def local(parent_entries, children, shift, child_map):
    rows_here, cols_here = parent_entries.shape
    grid_rows = lax.axis_size("row")
    grid_cols = lax.axis_size("col")
    half_grid = grid_cols // 2
    row_index = lax.axis_index("row")
    col_index = lax.axis_index("col")
    core = col_index % 2
    chip = col_index // 2
    chips = grid_cols // 2
    near = chips // 2
    child_now = col_index // half_grid
    child_rows, child_width = children.shape
    groups = child_rows // TILE
    half_rows = groups // 2
    slot_count = groups // grid_rows + 2
    row_blocks = rows_here // TILE
    lead_blocks = grid_cols // grid_rows
    eliminated = TILE * grid_cols
    cut = min(groups, grid_cols)
    most = min(2 * groups, 4 * slot_count)
    most += most % 2
    quota = cut // near

    row_map = child_map.reshape(2, groups, grid_rows).transpose(0, 2, 1)
    row_to = row_map % grid_rows
    ordinal = jnp.arange(groups)
    row_slot = jnp.sum(
        (row_to[:, :, :, None] == row_to[:, :, None, :]) & (ordinal[None, :] < ordinal[:, None]),
        axis=3,
        dtype=jnp.int32,
    )
    own_to = pick(pick(row_to, child_now), row_index)
    own_slot = pick(pick(row_slot, child_now), row_index)
    row_source = total(
        (own_to[None, None, :] == jnp.arange(grid_rows)[:, None, None])
        & (own_slot[None, None, :] == jnp.arange(slot_count)[None, :, None]),
        ordinal,
        2,
    ).reshape(-1)
    flat = grid_rows * groups
    here = (row_to == row_index).reshape(2, flat)
    spot = jnp.arange(flat)
    rank = jnp.sum(here[:, None, :] & (spot[None, :] < spot[:, None]), axis=2, dtype=jnp.int32)
    ranked = here[:, None, :] & (rank[:, None, :] == ordinal[None, :, None])
    slots = (row_slot + jnp.arange(grid_rows)[None, :, None] * slot_count).reshape(2, 1, flat)
    chosen = pick(total(ranked, slots, 2), child_now)
    row_lists = total(ranked, (row_map // grid_rows).reshape(2, 1, flat), 2)
    mine_chosen = lax.dynamic_slice_in_dim(chosen, core * half_rows, half_rows)
    other_chosen = lax.dynamic_slice_in_dim(chosen, (1 - core) * half_rows, half_rows)
    own_rows = pick(row_lists, child_now)
    far_rows = pick(row_lists, 1 - child_now)

    def halves(rows):
        return (
            lax.dynamic_slice_in_dim(rows, core * half_rows, half_rows),
            lax.dynamic_slice_in_dim(rows, (1 - core) * half_rows, half_rows),
        )

    col_map = child_map.reshape(2, groups, half_grid).transpose(0, 2, 1).reshape(grid_cols, groups)
    col_to = col_map % grid_cols
    hop = (col_to // 2) ^ (jnp.arange(grid_cols)[:, None] // 2)
    leads = col_map < grid_cols
    crosses = hop >= near
    before = ordinal[None, :] < ordinal[:, None]
    same = jnp.sum((hop[:, :, None] == hop[:, None, :]) & before, axis=2, dtype=jnp.int32)
    grade = jnp.where(leads, 0, jnp.where(crosses, jnp.where(same < quota, 1, 2), 3))
    key = grade * groups + ordinal
    position = jnp.sum(key[:, None, :] < key[:, :, None], axis=2, dtype=jnp.int32)
    own_position = pick(position, col_index)
    column_order = total(own_position[None, :] == ordinal[:, None], ordinal, 1)

    phase = jnp.where(leads, 0, jnp.where(position < cut, 1, 2))
    of_core = jnp.arange(grid_cols)[:, None] % 2
    list_key = ((phase * 2 + of_core) * groups + position).reshape(chips, 2 * groups)
    hop = hop.reshape(chips, 2 * groups)
    alike = hop[:, :, None] == hop[:, None, :]
    list_rank = jnp.sum(
        alike & (list_key[:, None, :] < list_key[:, :, None]), axis=2, dtype=jnp.int32
    )
    early_able = (phase < 2).reshape(chips, 2 * groups)
    able_count = jnp.sum(alike & early_able[:, None, :], axis=2, dtype=jnp.int32)
    is_early = early_able & (list_rank < LEADS)
    late_rank = list_rank - jnp.minimum(LEADS, able_count)
    place_in = (
        jnp.where(position < cut, 0, 2 * cut)
        + jnp.where(of_core == core, 0, jnp.where(position < cut, cut, groups - cut))
        + jnp.where(position < cut, position, position - cut)
    ).reshape(chips, 2 * groups)
    level = jnp.where(col_to == col_index, col_map // grid_cols, -1).reshape(chips, 2 * groups)
    chip_ids = jnp.arange(chips)

    def lists(rank, able, size):
        at = able[:, :, None] & (rank[:, :, None] == jnp.arange(size)[None, None, :])
        sends, gets = [], []
        for distance in range(chips):
            on = at & (hop == distance)[:, :, None]
            mine = on & (chip_ids == chip)[:, None, None]
            sends.append(total(mine, place_in[:, :, None], (0, 1)))
            theirs = on & ((chip_ids ^ distance) == chip)[:, None, None]
            gets.append(total(theirs, level[:, :, None] + 1, (0, 1)) - 1)
        return sends, gets

    early_sends, early_gets = lists(list_rank, is_early, LEADS)
    late_sends, late_gets = lists(late_rank, ~is_early, most)
    late_most = [
        jnp.max(jnp.where((hop == distance) & ~is_early, late_rank + 1, 0)) for distance in range(chips)
    ]

    child_blocks = children.reshape(groups, TILE, child_width)
    steps = jnp.arange(half_rows)

    def exchange(sent):
        shaped = sent.reshape(grid_rows, slot_count, TILE, sent.shape[2])
        return lax.all_to_all(shaped, "row", split_axis=0, concat_axis=0, tiled=True).reshape(sent.shape)

    def with_partner(arrived, other_chosen):
        got = flip(chosen_rows(arrived, other_chosen), "col", 1)
        return beside(arrived, mine_chosen, got)

    def tie(*values):
        return lax.optimization_barrier(values)

    [sent] = pack([child_blocks], row_source, [column_order[:cut]], grid_rows * slot_count)
    arrived = exchange(sent)
    if cut < groups:
        [sent] = pack([child_blocks], row_source, [column_order[cut:]], grid_rows * slot_count)
        arrived, sent = tie(arrived, sent)
    urgent = with_partner(arrived, other_chosen)
    tiles = [urgent]

    far, nearby = list(range(near, chips)), list(range(near))
    hops = far + nearby
    first = dict(zip(hops, pack([urgent], steps, [early_sends[x] for x in hops], half_rows)))
    if cut < groups:
        arrived = exchange(sent)
    first = {x: flip(first[x], "col", 2 * x) if x else first[x] for x in hops}
    turned = flip(jnp.stack([first[x] for x in hops]), "col", 1)
    first_pair = {x: turned[at] for at, x in enumerate(hops)}

    row_ids = (
        (jnp.arange(row_blocks) * grid_rows + row_index)[:, None] * TILE + jnp.arange(TILE)
    ).reshape(rows_here)
    panel_ids = jnp.where(jnp.arange(PAIR) < TILE, col_index * TILE + jnp.arange(PAIR), -1)
    panel = parent_entries[:, :PAIR] + jnp.where(
        row_ids[:, None] == panel_ids[None, :], shift[:, None], 0.0
    )
    own_halves, far_halves = halves(own_rows), halves(far_rows)
    parts, row_tables, tables = [], [], []
    for x in hops:
        for part, rows in zip((first[x], first_pair[x]), own_halves if x < near else far_halves):
            parts.append(part)
            row_tables.append(rows)
            tables.append(early_gets[x])
    corner, panel_t = add_leads(panel, parts, row_tables, tables, lead_blocks)
    corner = corner[:, :TILE].T
    corner, panel_t, later_chosen = tie(corner, panel_t, other_chosen)

    held = {0: panel_t}
    straight = [1 << bit for bit in range(1, grid_cols.bit_length() - 1)]
    for x in straight[::-1]:
        held[x] = flip(panel_t, "col", x)
    corner = unflip(gather_flips(corner, "col"), col_index)

    landed_late = min(LATE_CROSS, most)
    late, rest = {}, {}
    if cut < groups:
        tiles.append(with_partner(arrived, later_chosen))
    cuts = list(range(0, landed_late, -(-landed_late // 4) * 2)) + [landed_late]
    shares = list(zip(cuts, cuts[1:]))
    far_keys = [(x, low) for low, _ in shares for x in far]
    packed = pack(tiles, steps, [late_sends[x][low:high] for low, high in shares for x in far], half_rows)
    corner, *both = tie(corner, *packed, *[held[x] for x in straight])
    late.update(zip(far_keys, both))
    held.update(zip(straight, both[len(far_keys) :]))
    for key in far_keys:
        late[key] = flip(late[key], "col", 2 * key[0])

    for x in sorted(range(2, grid_cols, 2), key=lambda x: -(x & -x)):
        if x not in held:
            held[x] = flip(held[x ^ (x & -x)], "col", x & -x)
    corner = unflip(gather_flips(corner, "row"), row_index)
    leading = (
        corner.reshape(grid_rows, grid_cols, TILE, lead_blocks, TILE)
        .transpose(3, 0, 4, 1, 2)
        .reshape(eliminated, eliminated)
    )
    leading = (leading + leading.T) * 0.5
    mixes = [x for x in range(2, grid_cols, 2) if x not in straight]
    leading, late[far_keys[0]], *both = tie(leading, late[far_keys[0]], *[held[x] for x in mixes])
    held.update(zip(mixes, both))
    even = jnp.concatenate([held[x] for x in range(0, grid_cols, 2)], axis=0)
    odd = flip(even, "col", 1)
    moving = [x for x in nearby if x] + far
    near_sizes = [landed_late if x else most for x in nearby]
    packed = pack(tiles, steps, [late_sends[x][:n] for x, n in zip(nearby, near_sizes)], half_rows)

    def strips(pieces):
        here = lax.dynamic_slice_in_dim(pieces, (col_index // grid_rows) * cols_here, cols_here, 1)
        return jnp.where(row_index == col_index % grid_rows, here, 0.0)

    leading, strips_even, strips_odd, *packed = tie(leading, strips(even), strips(odd), *packed)
    matching = [lax.psum(strips_even, "row"), lax.psum(strips_odd, "row")]
    late.update(zip(nearby, packed))
    late.update({x: flip(late[x], "col", 2 * x) for x in nearby if x})

    pivot, inverse = factor_and_inverse(leading)
    inverse, after = tie(inverse, steps)
    if landed_late < most:
        rest = dict(zip(moving, pack(tiles, after, [late_sends[x][landed_late:] for x in moving], half_rows)))

    mixed = unflip(inverse.T.reshape(grid_cols, TILE, eliminated), col_index)
    mixes = [mixed[start::2].reshape(eliminated // 2, eliminated) for start in range(2)]

    def applied(a, b):
        return lax.dot_general(
            a,
            b,
            (((0,), (0,)), ((), ())),
            precision=lax.Precision.HIGH,
            preferred_element_type=jnp.float32,
        )

    factor = applied(even, mixes[0]) + applied(odd, mixes[1])
    factor = factor.reshape(lead_blocks, row_blocks // lead_blocks, TILE, eliminated)
    factor = factor.transpose(1, 0, 2, 3).reshape(rows_here, eliminated)
    factor_cols = applied(mixes[0], matching[0]) + applied(mixes[1], matching[1])
    wanted = [x for x in nearby if x] + far_keys[1:2]
    factor_cols, *both = tie(factor_cols, *[late[key] for key in wanted])
    late.update(zip(wanted, both))
    own_pivot = lax.dynamic_slice_in_dim(pivot, col_index * TILE, TILE, 1).reshape(
        lead_blocks, grid_rows, TILE, TILE
    )
    own_pivot = pick(own_pivot, row_index, 1).reshape(lead_blocks * TILE, TILE)
    own_factor = lax.dynamic_slice_in_dim(factor, col_index * TILE, TILE, 1)
    panel_out = jnp.concatenate([own_pivot, own_factor[lead_blocks * TILE :]], axis=0)
    panel_out = jnp.pad(panel_out, ((0, 0), (0, PAIR - TILE)))
    place = jnp.stack([row_index, col_index]).astype(jnp.int32)
    result = schur(parent_entries, factor, factor_cols, panel_out, shift, place, grid_rows, grid_cols)
    if len(far_keys) > 2:
        result, late[far_keys[2]] = tie(result, late[far_keys[2]])
    late_pair = {key: flip(late[key], "col", 1) for key in nearby}
    for side in range(2):
        result = extend_add(
            result,
            [(first, first_pair)[side][x] for x in nearby] + [(late, late_pair)[side][x] for x in nearby],
            own_halves[side],
            [early_gets[x] for x in nearby] + [late_gets[x][:n] for x, n in zip(nearby, near_sizes)],
            lead_blocks,
            1,
        )

    tables = [early_gets[x] for x in far] + [
        late_gets[x][low:high] for low, high in shares for x in far
    ]
    left = most - landed_late
    if left > 0:
        rounds = -(-left // LOOP_COLS)
        width = LOOP_COLS * TILE
        landing = {}
        keys = far_keys[3:]
        result, *settled = tie(result, *[late[key] for key in keys], *rest.values())
        late.update(zip(keys, settled))
        rest.update(zip(rest, settled[len(keys) :]))
        for x in moving:
            needed = (jnp.maximum(late_most[x] - landed_late, 0) + LOOP_COLS - 1) // LOOP_COLS
            source = jnp.pad(rest[x], ((0, 0), (0, 0), (0, rounds * width - left * TILE)))
            padding = jnp.full((rounds * LOOP_COLS - left,), -1, jnp.int32)
            table = jnp.concatenate([late_gets[x][landed_late:], padding])

            def body(index, carry):
                buffer, source = carry
                part = lax.dynamic_slice_in_dim(source, index * width, width, 2)
                part = flip(part, "col", 2 * x)
                return lax.dynamic_update_slice_in_dim(buffer, part, index * width, 2), source

            def body_near(index, carry):
                result, source = carry
                part = lax.dynamic_slice_in_dim(source, index * width, width, 2)
                part = flip(part, "col", 2 * x)
                wanted = [lax.dynamic_slice_in_dim(table, index * LOOP_COLS, LOOP_COLS)]
                for side, half in enumerate((part, flip(part, "col", 1))):
                    result = extend_add(result, [half], own_halves[side], wanted, lead_blocks, 1)
                return result, source

            if x in far:
                landing[x], _ = lax.fori_loop(0, needed, body, (jnp.zeros_like(source), source))
                tables.append(table)
            else:
                result, _ = lax.fori_loop(0, needed, body_near, (result, source))
        landing_pair = {x: flip(landing[x], "col", 1) for x in far}
    parts = [[first[x] for x in far] + [late[key] for key in far_keys]]
    parts.append([first_pair[x] for x in far] + [flip(late[key], "col", 1) for key in far_keys])
    if left > 0:
        parts[0] += landing.values()
        parts[1] += landing_pair.values()
    for side in range(2):
        result = extend_add(
            result,
            parts[side],
            far_halves[side],
            tables,
            lead_blocks,
            1,
        )
    return result


def solution(mesh):
    in_specs = (P("row", "col"), P("row", "col"), P("row"), P())
    out_specs = P("row", "col")
    return jax.shard_map(local, mesh=mesh, in_specs=in_specs, out_specs=out_specs, check_vma=False)
```

```python
import jax
import jax.numpy as jnp
from jax import lax
from jax.experimental import pallas as pl
from jax.experimental.pallas import tpu as pltpu
from jax.sharding import PartitionSpec as P

TILE = 64
PAIR = 2 * TILE
LOOP_COLS = 2
LEADS = 2
LATE_CROSS = 16
LATE_NEAR = 22
BLOCK = 128
SMALL = pl.CostEstimate(flops=1, transcendentals=0, bytes_accessed=1024)


def params(mib):
    return pltpu.CompilerParams(vmem_limit_bytes=mib * 1024 * 1024)


def total(mask, value, axis):
    return jnp.sum(jnp.where(mask, value, 0), axis=axis)


def pick(value, index, axis=0):
    return lax.dynamic_index_in_dim(value, index, axis=axis, keepdims=False)


def flip(value, axis, distance):
    pairs = [(i, i ^ distance) for i in range(lax.axis_size(axis))]
    return lax.ppermute(value, axis, pairs)


def gather_flips(value, axis):
    size = lax.axis_size(axis)
    held = {0: value}
    distance = size // 2
    while distance > 1:
        for x in list(held):
            held[x ^ distance] = flip(held[x], axis, distance)
        distance //= 2
    even = jnp.stack([held[x] for x in range(0, size, 2)])
    return jnp.stack([even, flip(even, axis, 1)], axis=1).reshape((size,) + value.shape)


def unflip(value, index):
    size = value.shape[0]
    rest = value.shape[1:]
    for bit in range(size.bit_length() - 1):
        shaped = value.reshape((size >> (bit + 1), 2, 1 << bit) + rest)
        value = jnp.where((index >> bit) & 1 == 1, shaped[:, ::-1], shaped).reshape((size,) + rest)
    return value


def lane_half(value, column, half):
    return jnp.where(column % 2 == half, value, pltpu.roll(value, TILE, 1))


def lane_pair(column):
    return pl.ds(pl.multiple_of((column // 2) * PAIR, PAIR), PAIR)


def pack(sources, row_table, column_tables, rows):
    counts = [table.shape[0] for table in column_tables]
    widths = [source.shape[2] // TILE for source in sources]
    given = len(sources)

    def body(row_ref, column_ref, *refs):
        low = lax.broadcasted_iota(jnp.int32, (TILE, PAIR), 1) < TILE
        at = 0
        for out_ref, count in zip(refs[given:], counts):
            for first in range(0, count, 2):
                halves = []
                for half in range(2):
                    column = column_ref[at]
                    at += 1
                    value = refs[0][0, :, lane_pair(jnp.minimum(column, widths[0] - 1))]
                    start = widths[0]
                    for ref, width in zip(refs[1:given], widths[1:]):
                        place = jnp.clip(column - start, 0, width - 1)
                        value = jnp.where(column >= start, ref[0, :, lane_pair(place)], value)
                        start += width
                    halves.append(lane_half(value, column, half))
                out_ref[0, :, first * TILE : (first + 2) * TILE] = jnp.where(low, halves[0], halves[1])

    return pl.pallas_call(
        body,
        out_shape=[jax.ShapeDtypeStruct((rows, TILE, count * TILE), jnp.float32) for count in counts],
        grid_spec=pltpu.PrefetchScalarGridSpec(
            num_scalar_prefetch=2,
            grid=(rows,),
            in_specs=[
                pl.BlockSpec((1, TILE, source.shape[2]), lambda j, row, column: (row[j], 0, 0))
                for source in sources
            ],
            out_specs=[
                pl.BlockSpec((1, TILE, count * TILE), lambda j, row, column: (j, 0, 0)) for count in counts
            ],
        ),
        compiler_params=params(40),
        cost_estimate=SMALL,
    )(row_table, jnp.concatenate(column_tables), *sources)


def beside(arrived, row_table, got):
    rows, _, width = got.shape

    def body(row_ref, own_ref, got_ref, out_ref):
        out_ref[0, :, :width] = own_ref[0]
        out_ref[0, :, width:] = got_ref[0]

    return pl.pallas_call(
        body,
        out_shape=jax.ShapeDtypeStruct((rows, TILE, 2 * width), jnp.float32),
        grid_spec=pltpu.PrefetchScalarGridSpec(
            num_scalar_prefetch=1,
            grid=(rows,),
            in_specs=[
                pl.BlockSpec((1, TILE, width), lambda j, row: (row[j], 0, 0)),
                pl.BlockSpec((1, TILE, width), lambda j, row: (j, 0, 0)),
            ],
            out_specs=pl.BlockSpec((1, TILE, 2 * width), lambda j, row: (j, 0, 0)),
        ),
        compiler_params=params(32),
        cost_estimate=SMALL,
    )(row_table, arrived, got)


def chosen_rows(arrived, row_table):
    rows = row_table.shape[0]
    width = arrived.shape[2]

    def body(row_ref, in_ref, out_ref):
        out_ref[...] = in_ref[...]

    return pl.pallas_call(
        body,
        out_shape=jax.ShapeDtypeStruct((rows, TILE, width), jnp.float32),
        grid_spec=pltpu.PrefetchScalarGridSpec(
            num_scalar_prefetch=1,
            grid=(rows,),
            in_specs=[pl.BlockSpec((1, TILE, width), lambda j, row: (row[j], 0, 0))],
            out_specs=pl.BlockSpec((1, TILE, width), lambda j, row: (j, 0, 0)),
        ),
        compiler_params=params(32),
        cost_estimate=SMALL,
    )(row_table, arrived)


def extend_add(front, parts, row_table, column_tables, skip_rows, skip_cols):
    rows = row_table.shape[0]
    width = front.shape[1]
    columns = jnp.concatenate(column_tables)

    def body(row_ref, column_ref, front_ref, *refs):
        out_ref = refs[-1]
        out_ref[...] = front_ref[...]

        @pl.when(row_ref[pl.program_id(0)] >= skip_rows)
        def _():
            upper = lax.broadcasted_iota(jnp.int32, (TILE, PAIR), 1) // TILE
            at = 0
            for ref in refs[:-1]:
                for q in range(ref.shape[2] // TILE):
                    column = column_ref[at]
                    at += 1

                    @pl.when(column >= skip_cols)
                    def _():
                        first = (q // 2) * PAIR
                        value = lane_half(ref[0, :, first : first + PAIR], column, q % 2)
                        out_ref[:, lane_pair(column)] += jnp.where(upper == column % 2, value, 0.0)

    return pl.pallas_call(
        body,
        out_shape=jax.ShapeDtypeStruct(front.shape, jnp.float32),
        grid_spec=pltpu.PrefetchScalarGridSpec(
            num_scalar_prefetch=2,
            grid=(rows,),
            in_specs=[pl.BlockSpec((TILE, width), lambda j, row, column: (row[j], 0))]
            + [
                pl.BlockSpec((1, TILE, part.shape[2]), lambda j, row, column: (j, 0, 0))
                for part in parts
            ],
            out_specs=pl.BlockSpec((TILE, width), lambda j, row, column: (row[j], 0)),
        ),
        input_output_aliases={2: 0},
        compiler_params=params(32),
        cost_estimate=SMALL,
    )(row_table, columns, front, *parts)


def add_leads(panel, parts, row_tables, tables, kinds):
    rows = parts[0].shape[0]
    count = panel.shape[0] // TILE
    row_table = jnp.concatenate(row_tables)
    table = jnp.concatenate(tables)
    order = [t for kind in range(kinds) for t in range(kind, count, kinds)]

    def body(row_ref, table_ref, panel_ref, *refs):
        top_ref, turned_ref, work = refs[-3:]
        work[...] = panel_ref[...]
        low = lax.broadcasted_iota(jnp.int32, (TILE, PAIR), 1) < TILE
        for at, ref in enumerate(refs[:-3]):
            first = table_ref[2 * at] == 0
            second = table_ref[2 * at + 1] == 0

            @pl.when(first | second)
            def _():
                for j in range(rows):
                    place = pl.ds(pl.multiple_of(row_ref[at * rows + j] * TILE, TILE), TILE)
                    value = ref[j]
                    value = jnp.where(first, value, pltpu.roll(value, TILE, 1))
                    work[place, :] += jnp.where(low, value, 0.0)

        top_ref[...] = work[: kinds * TILE, :]
        for at in range(0, count, 2):
            pair = [work[t * TILE : (t + 1) * TILE, :] for t in order[at : at + 2]]
            turned_ref[:, at * TILE : (at + 2) * TILE] = jnp.concatenate(pair, axis=0).T[:TILE]

    smem = pl.BlockSpec(memory_space=pltpu.SMEM)
    vmem = pl.BlockSpec(memory_space=pltpu.VMEM)
    return pl.pallas_call(
        body,
        out_shape=(
            jax.ShapeDtypeStruct((kinds * TILE, PAIR), jnp.float32),
            jax.ShapeDtypeStruct((TILE, panel.shape[0]), jnp.float32),
        ),
        in_specs=[smem, smem, vmem] + [vmem] * len(parts),
        out_specs=(vmem, vmem),
        scratch_shapes=[pltpu.VMEM(panel.shape, jnp.float32)],
        compiler_params=params(40),
        cost_estimate=SMALL,
    )(row_table, table, panel, *parts)


def factor_and_inverse(matrix):
    size = matrix.shape[0]
    block = min(BLOCK, size)

    def dot(a, b, transposed=False):
        return lax.dot_general(
            a,
            b,
            (((1,), (1 if transposed else 0,)), ((), ())),
            precision=lax.Precision.HIGHEST,
            preferred_element_type=jnp.float32,
        )

    def body(matrix_ref, factor_ref, inverse_ref, work):
        lane = lax.broadcasted_iota(jnp.int32, (block, block), 1)
        deep = lax.broadcasted_iota(jnp.int32, (block, block), 0)
        wide_lane = lax.broadcasted_iota(jnp.int32, (1, 2 * block), 1)
        down = lax.broadcasted_iota(jnp.int32, (block, 1), 0)
        factor_ref[...] = jnp.zeros_like(factor_ref)
        inverse_ref[...] = jnp.zeros_like(inverse_ref)
        for start in range(0, size, block):
            end = start + block
            column = matrix_ref[start:, start:end]
            if start:
                column = column - dot(factor_ref[start:, :start], factor_ref[start:end, :start], True)
            work[:, :block] = column[:block]
            work[:, block:] = jnp.where(lane == deep, 1.0, 0.0)

            def step(j, carry):
                row = work[pl.ds(j, 1), :]
                held = work[...]
                scale = 1.0 / jnp.sqrt(jnp.sum(jnp.where(wide_lane == j, row, 0.0), axis=1, keepdims=True))
                row = row * scale
                below = jnp.sum(jnp.where(lane == j, held[:, :block], 0.0), axis=1, keepdims=True)
                below = jnp.where(down > j, below * scale, 0.0)
                work[...] = jnp.where(down == j, row, held - below * row)
                return carry

            lax.fori_loop(0, block, step, 0)
            diagonal_inverse = jnp.where(lane <= deep, work[:, block:], 0.0)
            factor_ref[start:end, start:end] = jnp.where(lane >= deep, work[:, :block], 0.0).T
            if end < size:
                factor_ref[end:, start:end] = dot(column[block:], diagonal_inverse, True)
            inverse_ref[start:end, start:end] = diagonal_inverse
            if start:
                row = dot(factor_ref[start:end, :start], inverse_ref[:start, :start])
                inverse_ref[start:end, :start] = -dot(diagonal_inverse, row)

    vmem = pl.BlockSpec(memory_space=pltpu.VMEM)
    shape = jax.ShapeDtypeStruct(matrix.shape, jnp.float32)
    return pl.pallas_call(
        body,
        out_shape=(shape, shape),
        in_specs=[vmem],
        out_specs=(vmem, vmem),
        scratch_shapes=[pltpu.VMEM((block, 2 * block), jnp.float32)],
        compiler_params=params(40),
        cost_estimate=SMALL,
    )(matrix)


def schur(parent, factor, factor_cols, panel_out, shift, place, grid_rows, grid_cols):
    rows_here, cols_here = parent.shape
    depth = factor.shape[1]
    step = min(4 * TILE, rows_here)
    lead = (grid_cols // grid_rows) * TILE

    def split(value):
        high = lax.reduce_precision(value, 8, 7)
        return high.astype(jnp.bfloat16), (value - high).astype(jnp.bfloat16)

    f_high, f_low = split(factor)
    c_high, c_low = split(factor_cols)

    def body(place_ref, parent_ref, fh_ref, fl_ref, ch_ref, cl_ref, panel_ref, shift_ref, out_ref):
        def dot(a, b):
            return jnp.dot(a[...], b[...], preferred_element_type=jnp.float32)

        update = dot(fh_ref, ch_ref) + dot(fl_ref, ch_ref) + dot(fh_ref, cl_ref)
        row = pl.program_id(0) * step + lax.broadcasted_iota(jnp.int32, (step, 1), 0)
        column = lax.broadcasted_iota(jnp.int32, (1, cols_here), 1)
        row_id = ((row // TILE) * grid_rows + place_ref[0]) * TILE + row % TILE
        column_id = ((column // TILE) * grid_cols + place_ref[1]) * TILE + column % TILE
        value = parent_ref[...] - update + jnp.where(row_id == column_id, shift_ref[...], 0.0)
        out_ref[...] = jnp.where(row < lead, 0.0, value)
        first = jnp.where(
            lax.broadcasted_iota(jnp.int32, (step, PAIR), 1) < TILE, panel_ref[...], out_ref[:, :PAIR]
        )
        out_ref[:, :PAIR] = first

    whole = lambda j, place: (0, 0)
    block = lambda j, place: (j, 0)
    return pl.pallas_call(
        body,
        out_shape=jax.ShapeDtypeStruct(parent.shape, jnp.float32),
        grid_spec=pltpu.PrefetchScalarGridSpec(
            num_scalar_prefetch=1,
            grid=(rows_here // step,),
            in_specs=[
                pl.BlockSpec((step, cols_here), block),
                pl.BlockSpec((step, depth), block),
                pl.BlockSpec((step, depth), block),
                pl.BlockSpec((depth, cols_here), whole),
                pl.BlockSpec((depth, cols_here), whole),
                pl.BlockSpec((step, PAIR), block),
                pl.BlockSpec((step, 1), block),
            ],
            out_specs=pl.BlockSpec((step, cols_here), block),
        ),
        compiler_params=params(50),
        cost_estimate=SMALL,
    )(place, parent, f_high, f_low, c_high, c_low, panel_out, shift[:, None])


def local(parent_entries, children, shift, child_map):
    rows_here, cols_here = parent_entries.shape
    grid_rows = lax.axis_size("row")
    grid_cols = lax.axis_size("col")
    half_grid = grid_cols // 2
    row_index = lax.axis_index("row")
    col_index = lax.axis_index("col")
    core = col_index % 2
    chip = col_index // 2
    chips = grid_cols // 2
    near = chips // 2
    child_now = col_index // half_grid
    child_rows, child_width = children.shape
    groups = child_rows // TILE
    half_rows = groups // 2
    slot_count = groups // grid_rows + 2
    row_blocks = rows_here // TILE
    lead_blocks = grid_cols // grid_rows
    eliminated = TILE * grid_cols
    cut = min(groups, grid_cols)
    most = min(2 * groups, 4 * slot_count)
    most += most % 2
    quota = cut // near

    row_map = child_map.reshape(2, groups, grid_rows).transpose(0, 2, 1)
    row_to = row_map % grid_rows
    ordinal = jnp.arange(groups)
    row_slot = jnp.sum(
        (row_to[:, :, :, None] == row_to[:, :, None, :]) & (ordinal[None, :] < ordinal[:, None]),
        axis=3,
        dtype=jnp.int32,
    )
    own_to = pick(pick(row_to, child_now), row_index)
    own_slot = pick(pick(row_slot, child_now), row_index)
    row_source = total(
        (own_to[None, None, :] == jnp.arange(grid_rows)[:, None, None])
        & (own_slot[None, None, :] == jnp.arange(slot_count)[None, :, None]),
        ordinal,
        2,
    ).reshape(-1)
    flat = grid_rows * groups
    here = (row_to == row_index).reshape(2, flat)
    spot = jnp.arange(flat)
    rank = jnp.sum(here[:, None, :] & (spot[None, :] < spot[:, None]), axis=2, dtype=jnp.int32)
    ranked = here[:, None, :] & (rank[:, None, :] == ordinal[None, :, None])
    slots = (row_slot + jnp.arange(grid_rows)[None, :, None] * slot_count).reshape(2, 1, flat)
    chosen = pick(total(ranked, slots, 2), child_now)
    row_lists = total(ranked, (row_map // grid_rows).reshape(2, 1, flat), 2)
    mine_chosen = lax.dynamic_slice_in_dim(chosen, core * half_rows, half_rows)
    other_chosen = lax.dynamic_slice_in_dim(chosen, (1 - core) * half_rows, half_rows)
    own_rows = pick(row_lists, child_now)
    far_rows = pick(row_lists, 1 - child_now)

    def halves(rows):
        return (
            lax.dynamic_slice_in_dim(rows, core * half_rows, half_rows),
            lax.dynamic_slice_in_dim(rows, (1 - core) * half_rows, half_rows),
        )

    col_map = child_map.reshape(2, groups, half_grid).transpose(0, 2, 1).reshape(grid_cols, groups)
    col_to = col_map % grid_cols
    hop = (col_to // 2) ^ (jnp.arange(grid_cols)[:, None] // 2)
    leads = col_map < grid_cols
    crosses = hop >= near
    before = ordinal[None, :] < ordinal[:, None]
    same = jnp.sum((hop[:, :, None] == hop[:, None, :]) & before, axis=2, dtype=jnp.int32)
    grade = jnp.where(leads, 0, jnp.where(crosses, jnp.where(same < quota, 1, 2), 3))
    key = grade * groups + ordinal
    position = jnp.sum(key[:, None, :] < key[:, :, None], axis=2, dtype=jnp.int32)
    own_position = pick(position, col_index)
    column_order = total(own_position[None, :] == ordinal[:, None], ordinal, 1)

    phase = jnp.where(leads, 0, jnp.where(position < cut, 1, 2))
    of_core = jnp.arange(grid_cols)[:, None] % 2
    list_key = ((phase * 2 + of_core) * groups + position).reshape(chips, 2 * groups)
    hop = hop.reshape(chips, 2 * groups)
    alike = hop[:, :, None] == hop[:, None, :]
    list_rank = jnp.sum(
        alike & (list_key[:, None, :] < list_key[:, :, None]), axis=2, dtype=jnp.int32
    )
    early_able = (phase < 2).reshape(chips, 2 * groups)
    able_count = jnp.sum(alike & early_able[:, None, :], axis=2, dtype=jnp.int32)
    is_early = early_able & (list_rank < LEADS)
    late_rank = list_rank - jnp.minimum(LEADS, able_count)
    place_in = (
        jnp.where(position < cut, 0, 2 * cut)
        + jnp.where(of_core == core, 0, jnp.where(position < cut, cut, groups - cut))
        + jnp.where(position < cut, position, position - cut)
    ).reshape(chips, 2 * groups)
    level = jnp.where(col_to == col_index, col_map // grid_cols, -1).reshape(chips, 2 * groups)
    chip_ids = jnp.arange(chips)

    def lists(rank, able, size):
        at = able[:, :, None] & (rank[:, :, None] == jnp.arange(size)[None, None, :])
        sends, gets = [], []
        for distance in range(chips):
            on = at & (hop == distance)[:, :, None]
            mine = on & (chip_ids == chip)[:, None, None]
            sends.append(total(mine, place_in[:, :, None], (0, 1)))
            theirs = on & ((chip_ids ^ distance) == chip)[:, None, None]
            gets.append(total(theirs, level[:, :, None] + 1, (0, 1)) - 1)
        return sends, gets

    early_sends, early_gets = lists(list_rank, is_early, LEADS)
    late_sends, late_gets = lists(late_rank, ~is_early, most)
    late_most = [
        jnp.max(jnp.where((hop == distance) & ~is_early, late_rank + 1, 0)) for distance in range(chips)
    ]

    child_blocks = children.reshape(groups, TILE, child_width)
    steps = jnp.arange(half_rows)

    def exchange(sent):
        shaped = sent.reshape(grid_rows, slot_count, TILE, sent.shape[2])
        return lax.all_to_all(shaped, "row", split_axis=0, concat_axis=0, tiled=True).reshape(sent.shape)

    def with_partner(arrived, other_chosen):
        got = flip(chosen_rows(arrived, other_chosen), "col", 1)
        return beside(arrived, mine_chosen, got)

    def tie(*values):
        return lax.optimization_barrier(values)

    [sent] = pack([child_blocks], row_source, [column_order[:cut]], grid_rows * slot_count)
    arrived = exchange(sent)
    if cut < groups:
        [sent] = pack([child_blocks], row_source, [column_order[cut:]], grid_rows * slot_count)
        arrived, sent = tie(arrived, sent)
    urgent = with_partner(arrived, other_chosen)
    tiles = [urgent]

    far, nearby = list(range(near, chips)), list(range(near))
    hops = far + nearby
    first = dict(zip(hops, pack([urgent], steps, [early_sends[x] for x in hops], half_rows)))
    if cut < groups:
        arrived = exchange(sent)
    first = {x: flip(first[x], "col", 2 * x) if x else first[x] for x in hops}
    turned = flip(jnp.stack([first[x] for x in hops]), "col", 1)
    first_pair = {x: turned[at] for at, x in enumerate(hops)}

    row_ids = (
        (jnp.arange(row_blocks) * grid_rows + row_index)[:, None] * TILE + jnp.arange(TILE)
    ).reshape(rows_here)
    panel_ids = jnp.where(jnp.arange(PAIR) < TILE, col_index * TILE + jnp.arange(PAIR), -1)
    panel = parent_entries[:, :PAIR] + jnp.where(
        row_ids[:, None] == panel_ids[None, :], shift[:, None], 0.0
    )
    own_halves, far_halves = halves(own_rows), halves(far_rows)
    parts, row_tables, tables = [], [], []
    for x in hops:
        for part, rows in zip((first[x], first_pair[x]), own_halves if x < near else far_halves):
            parts.append(part)
            row_tables.append(rows)
            tables.append(early_gets[x])
    corner, panel_t = add_leads(panel, parts, row_tables, tables, lead_blocks)
    corner = corner[:, :TILE].T

    held = {0: panel_t}
    straight = [1 << bit for bit in range(1, grid_cols.bit_length() - 1)]
    for x in straight[::-1]:
        held[x] = flip(panel_t, "col", x)
    corner = unflip(gather_flips(corner, "col"), col_index)
    corner, later_chosen = tie(corner, other_chosen)

    landed_late = min(LATE_CROSS, most)
    late, rest = {}, {}
    if cut < groups:
        tiles.append(with_partner(arrived, later_chosen))
    cuts = {x: min(6 if x == near else 10, landed_late // 4 * 2) for x in far}
    shares = [(x, 0, cuts[x]) for x in far] + [(x, cuts[x], landed_late) for x in far]
    far_keys = [(x, low) for x, low, _ in shares]
    packed = pack(tiles, steps, [late_sends[x][low:high] for x, low, high in shares], half_rows)
    corner, *both = tie(corner, *packed, *[held[x] for x in straight])
    late.update(zip(far_keys, both))
    held.update(zip(straight, both[len(far_keys) :]))
    for key in far_keys:
        late[key] = flip(late[key], "col", 2 * key[0])

    for x in sorted(range(2, grid_cols, 2), key=lambda x: -(x & -x)):
        if x not in held:
            held[x] = flip(held[x ^ (x & -x)], "col", x & -x)
    corner = unflip(gather_flips(corner, "row"), row_index)
    leading = (
        corner.reshape(grid_rows, grid_cols, TILE, lead_blocks, TILE)
        .transpose(3, 0, 4, 1, 2)
        .reshape(eliminated, eliminated)
    )
    leading = (leading + leading.T) * 0.5
    mixes = [x for x in range(2, grid_cols, 2) if x not in straight]
    leading, late[far_keys[0]], *both = tie(leading, late[far_keys[0]], *[held[x] for x in mixes])
    held.update(zip(mixes, both))
    even = jnp.concatenate([held[x] for x in range(0, grid_cols, 2)], axis=0)
    odd = flip(even, "col", 1)
    moving = [x for x in nearby if x] + far
    near_sizes = [min(LATE_NEAR, most) if x else most for x in nearby]
    sizes = dict(zip(nearby, near_sizes)) | {x: landed_late for x in far}
    packed = pack(tiles, steps, [late_sends[x][:n] for x, n in zip(nearby, near_sizes)], half_rows)

    def strips(pieces):
        here = lax.dynamic_slice_in_dim(pieces, (col_index // grid_rows) * cols_here, cols_here, 1)
        return jnp.where(row_index == col_index % grid_rows, here, 0.0)

    leading, strips_even, strips_odd, *packed = tie(leading, strips(even), strips(odd), *packed)
    matching = [lax.psum(strips_even, "row"), lax.psum(strips_odd, "row")]
    late.update(zip(nearby, packed))
    late.update({x: flip(late[x], "col", 2 * x) for x in nearby if x})

    pivot, inverse = factor_and_inverse(leading)

    mixed = unflip(inverse.T.reshape(grid_cols, TILE, eliminated), col_index)
    mixes = [mixed[start::2].reshape(eliminated // 2, eliminated) for start in range(2)]
    mixes, matching = tie(mixes, matching)

    def applied(a, b):
        return lax.dot_general(
            a,
            b,
            (((0,), (0,)), ((), ())),
            precision=lax.Precision.HIGH,
            preferred_element_type=jnp.float32,
        )

    factor = applied(even, mixes[0]) + applied(odd, mixes[1])
    factor = factor.reshape(lead_blocks, row_blocks // lead_blocks, TILE, eliminated)
    factor = factor.transpose(1, 0, 2, 3).reshape(rows_here, eliminated)
    factor_cols = applied(mixes[0], matching[0]) + applied(mixes[1], matching[1])
    factor_cols, late[far_keys[1]] = tie(factor_cols, late[far_keys[1]])
    own_pivot = lax.dynamic_slice_in_dim(pivot, col_index * TILE, TILE, 1).reshape(
        lead_blocks, grid_rows, TILE, TILE
    )
    own_pivot = pick(own_pivot, row_index, 1).reshape(lead_blocks * TILE, TILE)
    own_factor = lax.dynamic_slice_in_dim(factor, col_index * TILE, TILE, 1)
    panel_out = jnp.concatenate([own_pivot, own_factor[lead_blocks * TILE :]], axis=0)
    panel_out = jnp.pad(panel_out, ((0, 0), (0, PAIR - TILE)))
    place = jnp.stack([row_index, col_index]).astype(jnp.int32)
    result = schur(parent_entries, factor, factor_cols, panel_out, shift, place, grid_rows, grid_cols)
    result, after, *both = tie(result, steps, *[late[key] for key in far_keys[2:4]])
    late.update(zip(far_keys[2:4], both))
    moving = [x for x in moving if sizes[x] < most]
    if moving:
        rest = dict(zip(moving, pack(tiles, after, [late_sends[x][sizes[x] :] for x in moving], half_rows)))
        result, *both = tie(result, *rest.values())
        rest.update(zip(moving, both))
    width = LOOP_COLS * TILE

    def rounds_of(x):
        needed = (jnp.maximum(late_most[x] - sizes[x], 0) + LOOP_COLS - 1) // LOOP_COLS
        spare = -(most - sizes[x]) % LOOP_COLS
        source = jnp.pad(rest[x], ((0, 0), (0, 0), (0, spare * TILE)))
        return needed, source, jnp.concatenate([late_gets[x][sizes[x] :], jnp.full((spare,), -1, jnp.int32)])

    def moved(source, index, x):
        return flip(lax.dynamic_slice_in_dim(source, index * width, width, 2), "col", 2 * x)

    tables = [early_gets[x] for x in far] + [late_gets[x][low:high] for x, low, high in shares]
    parts = [[first[x] for x in far] + [late[key] for key in far_keys]]
    parts.append([first_pair[x] for x in far] + [flip(late[key], "col", 1) for key in far_keys])
    for x in [x for x in far if x in moving]:
        needed, source, table = rounds_of(x)

        def collect(index, carry):
            buffer, source = carry
            part = moved(source, index, x)
            return lax.dynamic_update_slice_in_dim(buffer, part, index * width, 2), source

        landing, _ = lax.fori_loop(0, needed, collect, (jnp.zeros_like(source), source))
        tables.append(table)
        parts[0].append(landing)
        parts[1].append(flip(landing, "col", 1))
    result = extend_add(result, parts[0], far_halves[0], tables, lead_blocks, 1)
    wanted = [x for x in nearby if x]
    result, *both = tie(result, *[late[x] for x in wanted])
    late.update(zip(wanted, both))
    late_pair = {x: flip(late[x], "col", 1) for x in nearby}
    result = extend_add(result, parts[1], far_halves[1], tables, lead_blocks, 1)

    tables = [early_gets[x] for x in nearby] + [late_gets[x][: sizes[x]] for x in nearby]
    parts = [[first[x] for x in nearby] + [late[x] for x in nearby]]
    parts.append([first_pair[x] for x in nearby] + [late_pair[x] for x in nearby])
    for side in range(2):
        result = extend_add(result, parts[side], own_halves[side], tables, lead_blocks, 1)
    for x in [x for x in nearby if x in moving]:
        needed, source, table = rounds_of(x)

        def add(index, carry):
            result, source = carry
            part = moved(source, index, x)
            wanted = [lax.dynamic_slice_in_dim(table, index * LOOP_COLS, LOOP_COLS)]
            for side, half in enumerate((part, flip(part, "col", 1))):
                result = extend_add(result, [half], own_halves[side], wanted, lead_blocks, 1)
            return result, source

        result, _ = lax.fori_loop(0, needed, add, (result, source))
    return result


def solution(mesh):
    in_specs = (P("row", "col"), P("row", "col"), P("row"), P())
    out_specs = P("row", "col")
    return jax.shard_map(local, mesh=mesh, in_specs=in_specs, out_specs=out_specs, check_vma=False)
```
